32 devices in a mesh: rows: 8 (over z, y), vecs: 4 (over x, core).
Axes of the slice: x: 2, y: 2, z: 4, core: 2. Of those that a mesh axis runs over, the one named last changes fastest.
Arguments:
- vectors: bfloat16 [32768, 1024], P('rows', 'vecs'), may hold values from -6 to 6, as said below
- blocks: bfloat16 [256, 5, 128, 128], P('rows'), may hold values from -0.25 to 0.25
- columns: int32 [256, 5], P('rows'), may hold values from 0 to 255, as said below
Outputs:
- basis: float32 [32768, 1024], P('rows', 'vecs')
The draws below stay inside these ranges and needn't reach their ends.
Inputs may be any that keep to these rules, and one draw needn't show every extreme that they name: Each block row i names 5 block columns of the form i + d clipped to 0 .. 255, with distinct d in -8 .. 8; near the grid's ends some may repeat. `vectors`: entries of order one.
All inputs are finite; a program needn't handle non-finite values.
Results may differ from the reference program's by a relative error of at most 0.0075.
Values may be sent and summed in bfloat16 or wider, within the bound.
A program may use at most 128 MiB of HBM per device.

```python
import jax
import jax.numpy as jnp
from jax import lax

B = 128
K = 1024
NNZ = 5
DEGREE = 4
BR_DEV = 32
REACH = 8
NB = 256
NROWS = 32768
N_ROWS = 8


def draw_columns(key, part):
    breadth = 2 * REACH + 1
    row_ids = jnp.arange(NB, dtype=jnp.int32)[:, None]
    scores = jax.random.randint(key, (NB, breadth), 0, 1 << 20, dtype=jnp.int32) * breadth + jnp.arange(breadth, dtype=jnp.int32)[None, :]
    values, chosen = lax.top_k(scores, NNZ)
    picked = jnp.clip(row_ids + chosen.astype(jnp.int32) - REACH, 0, NB - 1)
    return picked.astype(jnp.int32)


def draw_vectors(key, part):
    first_key = jax.random.fold_in(key, 11)
    third_key = jax.random.fold_in(key, 13)
    entries = jax.random.normal(first_key, (NROWS, K), jnp.float32)
    common = jax.random.normal(third_key, (NROWS, 1), jnp.float32)
    values = jnp.clip(entries + 0.4 * common, -6.0, 6.0)
    return values.astype(jnp.bfloat16)


def block_scale(rng, shape, shards, smallest, largest):
    loudness = 1.0
    for axis_at, shards_of in shards:
        draws = jax.random.uniform(jax.random.fold_in(jax.random.fold_in(rng, 6), axis_at), (shards_of,), jnp.float32, smallest / len(shards), largest / len(shards))
        loudness = loudness * jnp.repeat(jnp.exp(draws), shape[axis_at] // shards_of).reshape((-1,) + (1,) * (len(shape) - 1 - axis_at))
    return loudness


def bell_draw(key, shape, width, reach, shards=(), held_as=jnp.bfloat16):
    level = block_scale(key, shape, shards, -0.22, 0.18) if shards else 1.0
    values = jax.random.normal(key, shape, jnp.float32) * width * level
    return jnp.minimum(jnp.maximum(values, -reach), reach).astype(held_as)


def setup_inputs(seed: int = 0) -> dict:
    splits = jax.random.split(jax.random.key(seed), 4)
    vectors = draw_vectors(jax.random.fold_in(splits[3], 71), 0)
    blocks = bell_draw(splits[1], (NB, NNZ, B, B), (NNZ * B) ** -0.5, 0.25, ((0, 8),))
    columns = draw_columns(jax.random.fold_in(splits[3], 71), 0)
    return dict(vectors=vectors, blocks=blocks, columns=columns)


filter_center = 0.25
filter_radius = 1.25

def product(vec_bf, blocks, columns):
    stacked = vec_bf.reshape(NB, B, K)
    cols_slab = columns.reshape(N_ROWS, BR_DEV, NNZ)
    blocks_slab = blocks.reshape(N_ROWS, BR_DEV, NNZ, B, B)

    def one_slab(pair):
        slab_cols, slab_blocks = pair
        picked = stacked[slab_cols].astype(jnp.float32)
        return jnp.einsum('rjab,rjbk->rak', slab_blocks.astype(jnp.float32), picked)
    result = lax.map(one_slab, (cols_slab, blocks_slab))
    return result.reshape(NROWS, K)

def reference(vectors, blocks, columns):
    older = vectors.astype(jnp.float32)
    current = (product(vectors, blocks, columns) - filter_center * older) / filter_radius
    for iteration in range(1, DEGREE):
        rounded = current.astype(jnp.bfloat16)
        newer = 2.0 * (product(rounded, blocks, columns) - filter_center * current) / filter_radius - older
        older = current
        current = newer
    final = current.astype(jnp.bfloat16)
    gram_matrix = jnp.dot(final.T.astype(jnp.float32), final.astype(jnp.float32), preferred_element_type=jnp.float32) / NROWS
    lower = jnp.linalg.cholesky(gram_matrix)
    identity = jnp.eye(K, dtype=jnp.float32)
    inverse = lax.linalg.triangular_solve(lower, identity, left_side=True, lower=True)
    inverse_high = inverse.astype(jnp.bfloat16)
    inverse_low = (inverse - inverse_high.astype(jnp.float32)).astype(jnp.bfloat16)
    first = jnp.dot(final.astype(jnp.float32), inverse_high.T.astype(jnp.float32), preferred_element_type=jnp.float32)
    second = jnp.dot(final.astype(jnp.float32), inverse_low.T.astype(jnp.float32), preferred_element_type=jnp.float32)
    return first + second
```

```python
import functools

import jax
import jax.numpy as jnp
from jax import lax
from jax.experimental import pallas as pl
from jax.experimental.pallas import tpu as pltpu
from jax.sharding import PartitionSpec as P

DEGREE = 4

filter_center = 0.25
filter_radius = 1.25

HIGHEST = lax.Precision.HIGHEST
VMEM_LIMIT = 56 * 1024 * 1024


def step_kernel(group, n_pieces, kind, emit_f32, index_ref, *refs):
    pieces = refs[:n_pieces]
    blocks_ref = refs[n_pieces]
    rest = refs[n_pieces + 1 :]
    if kind == "first":
        (cur_ref, *outs), old_ref = rest, None
    else:
        cur_ref, old_ref, *outs = rest
    *outs, window = outs
    step = pl.program_id(0)
    size_b = blocks_ref.shape[2]
    nnz = blocks_ref.shape[1]

    @pl.when(step == 0)
    def _():
        start = 0
        for piece in pieces:
            count = piece.shape[0]
            window[start : start + count, :] = piece[...]
            start += count

    for g in range(group):
        acc = None
        for j in range(nnz):
            at = pl.multiple_of(index_ref[(step * group + g) * nnz + j] * size_b, size_b)
            part = jnp.dot(
                blocks_ref[g, j], window[pl.ds(at, size_b), :], preferred_element_type=jnp.float32
            )
            acc = part if acc is None else acc + part
        rows = slice(g * size_b, (g + 1) * size_b)
        cur = cur_ref[rows, :].astype(jnp.float32)
        new = (acc - filter_center * cur) * (1.0 / filter_radius)
        if kind != "first":
            new = 2.0 * new - old_ref[rows, :].astype(jnp.float32)
        outs[0][rows, :] = new.astype(jnp.bfloat16)
        if emit_f32:
            outs[1][rows, :] = new


def chebyshev_step(index, pieces, blocks, row_of, count, cur, old, kind, emit_f32):
    size_b, nnz = blocks.shape[2], blocks.shape[1]
    width = pieces[0].shape[1]
    group = 4 if count % 4 == 0 else 1
    whole = lambda i, ix: (0, 0)
    part = lambda i, ix: (i, 0)
    tall = (group * size_b, width)
    in_specs = [pl.BlockSpec(p.shape, whole) for p in pieces]
    in_specs.append(
        pl.BlockSpec((group, nnz, size_b, size_b), lambda i, ix: (row_of(i, group), 0, 0, 0))
    )
    operands = list(pieces) + [blocks, cur]
    in_specs.append(pl.BlockSpec(tall, part))
    if kind != "first":
        operands.append(old)
        in_specs.append(pl.BlockSpec(tall, part))
    rows = count * size_b
    out_shape = [jax.ShapeDtypeStruct((rows, width), jnp.bfloat16)]
    if emit_f32:
        out_shape.append(jax.ShapeDtypeStruct((rows, width), jnp.float32))
    window_rows = sum(p.shape[0] for p in pieces)
    return pl.pallas_call(
        functools.partial(step_kernel, group, len(pieces), kind, emit_f32),
        grid_spec=pltpu.PrefetchScalarGridSpec(
            num_scalar_prefetch=1,
            grid=(count // group,),
            in_specs=in_specs,
            out_specs=[pl.BlockSpec(tall, part) for _ in out_shape],
            scratch_shapes=[pltpu.VMEM((window_rows, width), jnp.bfloat16)],
        ),
        out_shape=out_shape,
        compiler_params=pltpu.CompilerParams(vmem_limit_bytes=VMEM_LIMIT),
        cost_estimate=pl.CostEstimate(
            flops=2 * rows * nnz * size_b * width,
            bytes_accessed=rows * nnz * size_b * 2 + rows * width * 16,
            transcendentals=0,
        ),
    )(index, *operands)


def factor_block(block):
    size = block.shape[0]
    tiles = [block[8 * t : 8 * (t + 1), :] for t in range(size // 8)]
    lane = lax.broadcasted_iota(jnp.int32, (8, size), 1)
    sub = lax.broadcasted_iota(jnp.int32, (8, size), 0)
    for j in range(size):
        first, r = divmod(j, 8)
        at_j = lane == j
        row = jnp.broadcast_to(tiles[first][r : r + 1, :], (8, size))
        pivot = jnp.broadcast_to(row[:, j : j + 1], (8, size))
        scale = lax.rsqrt(pivot)
        scale = scale * (1.5 - 0.5 * (pivot * scale) * scale)
        scaled = jnp.where(at_j, 1.0, row) * scale
        twice = scaled * scale
        for t in range(first, size // 8):
            tile = tiles[t]
            column = jnp.broadcast_to(tile[:, j : j + 1], (8, size))
            new = jnp.where(at_j, 0.0, tile) - column * twice
            if t == first:
                new = jnp.where(sub > r, new, jnp.where(sub == r, scaled, tile))
            tiles[t] = new
    return jnp.concatenate(tiles, axis=0)


def inverse_kernel(size, total_rows, gram_ref, out_ref, work, factor):
    full = gram_ref.shape[0]
    count = full // size
    work[...] = gram_ref[...] / total_rows

    @pl.loop(0, count)
    def _(k):
        at = pl.multiple_of(k * size, size)
        done = factor_block(work[pl.ds(at, size), pl.ds(at, size)])
        down = lax.broadcasted_iota(jnp.int32, (size, size), 0)
        across = lax.broadcasted_iota(jnp.int32, (size, size), 1)
        factor[...] = jnp.where(across <= down, done, 0.0)
        for c in range(count):
            own = slice(c * size, (c + 1) * size)
            below = slice((c + 1) * size, full)

            @pl.when(k == c)
            def _():
                lower_inv = factor[...]
                left = slice(0, c * size)
                if c > 0:
                    out_ref[own, left] = jnp.dot(
                        lower_inv, work[own, left], precision=HIGHEST,
                        preferred_element_type=jnp.float32,
                    )
                out_ref[own, own] = lower_inv
                if c + 1 < count:
                    out_ref[own, below] = jnp.zeros((size, full - (c + 1) * size), jnp.float32)
                    right = jnp.dot(
                        lower_inv, work[own, below], precision=HIGHEST,
                        preferred_element_type=jnp.float32,
                    )
                    down_left = (((0,), (0,)), ((), ()))
                    work[below, below] -= lax.dot_general(
                        right, right, down_left, precision=HIGHEST,
                        preferred_element_type=jnp.float32,
                    )
                    known = slice(0, (c + 1) * size)
                    change = lax.dot_general(
                        right, out_ref[own, known], down_left, precision=HIGHEST,
                        preferred_element_type=jnp.float32,
                    )
                    if c > 0:
                        work[below, left] -= change[:, : c * size]
                    work[below, own] = -change[:, c * size :]


def inverse_factor(gram, total_rows):
    full = gram.shape[0]
    size = 128
    return pl.pallas_call(
        functools.partial(inverse_kernel, size, total_rows),
        out_shape=jax.ShapeDtypeStruct((full, full), jnp.float32),
        in_specs=[pl.BlockSpec(memory_space=pltpu.VMEM)],
        out_specs=pl.BlockSpec(memory_space=pltpu.VMEM),
        scratch_shapes=[
            pltpu.VMEM((full, full), jnp.float32),
            pltpu.VMEM((size, size), jnp.float32),
        ],
        compiler_params=pltpu.CompilerParams(vmem_limit_bytes=VMEM_LIMIT),
        cost_estimate=pl.CostEstimate(
            flops=40 * full * full * full, bytes_accessed=8 * full * full, transcendentals=full
        ),
    )(gram)


def split_apply(left_bf, factor):
    factor_high = factor.astype(jnp.bfloat16)
    factor_low = (factor - factor_high.astype(jnp.float32)).astype(jnp.bfloat16)
    first = jnp.dot(left_bf, factor_high.T, preferred_element_type=jnp.float32)
    second = jnp.dot(left_bf, factor_low.T, preferred_element_type=jnp.float32)
    return first + second


def filtered_block(vectors, blocks, columns):
    block_rows, nnz, size_b = blocks.shape[:3]
    reach = block_rows // 4
    edge = reach * size_b
    first_row = lax.axis_index("rows") * block_rows
    local = columns - first_row
    edges_index = jnp.concatenate([local[:reach], local[block_rows - reach :]], axis=0) + reach
    edges_index = edges_index.reshape(-1)
    inner_index = local[reach : block_rows - reach].reshape(-1)
    inner_rows = block_rows - 2 * reach

    axis_size = lax.axis_size("rows")
    up = [(i, i + 1) for i in range(axis_size - 1)]
    down = [(j, i) for i, j in up]

    def inner_of(i, group):
        return i + reach // group

    def edges_of(i, group):
        return jnp.where(i < reach // group, i, i + inner_rows // group)

    def halves(array):
        return jnp.concatenate([array[:edge], array[-edge:]], axis=0), array[edge:-edge]

    cur_edges, cur_inner = halves(vectors)
    bf_edges, bf_inner = cur_edges, cur_inner
    old_edges = old_inner = None
    for iteration in range(DEGREE):
        kind = "first" if iteration == 0 else "next"
        emit_f32 = iteration < DEGREE - 1
        low, high = bf_edges[:edge], bf_edges[edge:]
        before = lax.ppermute(high, "rows", up)
        after = lax.ppermute(low, "rows", down)
        own = [low, bf_inner, high]
        new_inner = chebyshev_step(
            inner_index, own, blocks, inner_of, inner_rows, cur_inner, old_inner, kind, emit_f32
        )
        new_edges = chebyshev_step(
            edges_index, [before] + own + [after], blocks, edges_of, 2 * reach,
            cur_edges, old_edges, kind, emit_f32,
        )
        old_edges, old_inner = cur_edges, cur_inner
        bf_edges, bf_inner = new_edges[0], new_inner[0]
        if emit_f32:
            cur_edges, cur_inner = new_edges[1], new_inner[1]
    return jnp.concatenate([bf_edges[:edge], bf_inner, bf_edges[edge:]], axis=0)


def shards(vectors, blocks, columns):
    total_rows = vectors.shape[0] * lax.axis_size("rows")
    final = filtered_block(vectors, blocks, columns)
    panel_width = final.shape[1]
    whole_block = lax.all_gather(final, "vecs", axis=1, tiled=True)
    panel = lax.dot_general(
        final, whole_block, (((0,), (0,)), ((), ())), preferred_element_type=jnp.float32
    )
    summed = lax.psum_scatter(panel, "rows", scatter_dimension=0, tiled=True)
    gram = lax.all_gather(summed, ("vecs", "rows"), axis=0, tiled=True)
    inverse = inverse_factor(gram, total_rows)
    own_rows = lax.dynamic_slice_in_dim(
        inverse, lax.axis_index("vecs") * panel_width, panel_width, 0
    )
    return split_apply(whole_block, own_rows)


def solution(mesh):
    in_specs = (P("rows", "vecs"), P("rows", None, None, None), P("rows", None))
    out_specs = P("rows", "vecs")
    return jax.shard_map(shards, mesh=mesh, in_specs=in_specs, out_specs=out_specs, check_vma=False)
```

```python
import functools

import jax
import jax.numpy as jnp
from jax import lax
from jax.experimental import pallas as pl
from jax.experimental.pallas import tpu as pltpu
from jax.sharding import PartitionSpec as P

DEGREE = 4

filter_center = 0.25
filter_radius = 1.25

HIGHEST = lax.Precision.HIGHEST
VMEM_LIMIT = 56 * 1024 * 1024
PIVOTS = 8


def step_kernel(group, n_pieces, kind, emit_f32, index_ref, *refs):
    pieces = refs[:n_pieces]
    blocks_ref = refs[n_pieces]
    rest = refs[n_pieces + 1 :]
    if kind == "first":
        (cur_ref, *outs), old_ref = rest, None
    else:
        cur_ref, old_ref, *outs = rest
    *outs, window = outs
    step = pl.program_id(0)
    size_b = blocks_ref.shape[2]
    nnz = blocks_ref.shape[1]

    @pl.when(step == 0)
    def _():
        start = 0
        for piece in pieces:
            count = piece.shape[0]
            window[start : start + count, :] = piece[...]
            start += count

    for g in range(group):
        acc = None
        for j in range(nnz):
            at = pl.multiple_of(index_ref[(step * group + g) * nnz + j] * size_b, size_b)
            part = jnp.dot(
                blocks_ref[g, j], window[pl.ds(at, size_b), :], preferred_element_type=jnp.float32
            )
            acc = part if acc is None else acc + part
        rows = slice(g * size_b, (g + 1) * size_b)
        cur = cur_ref[rows, :].astype(jnp.float32)
        new = (acc - filter_center * cur) * (1.0 / filter_radius)
        if kind != "first":
            new = 2.0 * new - old_ref[rows, :].astype(jnp.float32)
        outs[0][rows, :] = new.astype(jnp.bfloat16)
        if emit_f32:
            outs[1][rows, :] = new


def chebyshev_step(index, pieces, blocks, row_of, count, cur, old, kind, emit_f32):
    size_b, nnz = blocks.shape[2], blocks.shape[1]
    width = pieces[0].shape[1]
    group = 4 if count % 4 == 0 else 1
    whole = lambda i, ix: (0, 0)
    part = lambda i, ix: (i, 0)
    tall = (group * size_b, width)
    in_specs = [pl.BlockSpec(p.shape, whole) for p in pieces]
    in_specs.append(
        pl.BlockSpec((group, nnz, size_b, size_b), lambda i, ix: (row_of(i, group), 0, 0, 0))
    )
    operands = list(pieces) + [blocks, cur]
    in_specs.append(pl.BlockSpec(tall, part))
    if kind != "first":
        operands.append(old)
        in_specs.append(pl.BlockSpec(tall, part))
    rows = count * size_b
    out_shape = [jax.ShapeDtypeStruct((rows, width), jnp.bfloat16)]
    if emit_f32:
        out_shape.append(jax.ShapeDtypeStruct((rows, width), jnp.float32))
    window_rows = sum(p.shape[0] for p in pieces)
    return pl.pallas_call(
        functools.partial(step_kernel, group, len(pieces), kind, emit_f32),
        grid_spec=pltpu.PrefetchScalarGridSpec(
            num_scalar_prefetch=1,
            grid=(count // group,),
            in_specs=in_specs,
            out_specs=[pl.BlockSpec(tall, part) for _ in out_shape],
            scratch_shapes=[pltpu.VMEM((window_rows, width), jnp.bfloat16)],
        ),
        out_shape=out_shape,
        compiler_params=pltpu.CompilerParams(vmem_limit_bytes=VMEM_LIMIT),
        cost_estimate=pl.CostEstimate(
            flops=2 * rows * nnz * size_b * width,
            bytes_accessed=rows * nnz * size_b * 2 + rows * width * 16,
            transcendentals=0,
        ),
    )(index, *operands)


def factor_block(block):
    size = block.shape[0]
    tiles = [block[8 * t : 8 * (t + 1), :] for t in range(size // 8)]
    lane = lax.broadcasted_iota(jnp.int32, (8, size), 1)
    sub = lax.broadcasted_iota(jnp.int32, (8, size), 0)

    def spread(array):
        return jnp.broadcast_to(array, (8, size))

    for j in range(0, size, PIVOTS):
        first, r = divmod(j, 8)
        each = range(PIVOTS)
        at_any = jnp.logical_and(lane >= j, lane < j + PIVOTS)
        head = tiles[first]
        cols = [spread(head[:, j + a : j + a + 1]) for a in each]
        pivots = [[spread(cols[a][r + b : r + b + 1, :]) for a in range(b + 1)] for b in each]
        rows = [jnp.where(at_any, 0.0, spread(head[r + a : r + a + 1, :])) for a in each]
        rows = [jnp.where(lane == j + a, 1.0, rows[a]) for a in each]
        over, ratio = [], {}
        for a in each:
            over.append(1.0 / pivots[a][a])
            for b in range(a + 1, PIVOTS):
                ratio[b, a] = pivots[b][a] * over[a]
                for c in range(a + 1, b + 1):
                    pivots[b][c] = pivots[b][c] - ratio[b, a] * pivots[c][a]
                rows[b] = rows[b] - ratio[b, a] * rows[a]
        use = [None] * PIVOTS
        for a in reversed(each):
            use[a] = rows[a] * over[a]
            for b in range(a + 1, PIVOTS):
                use[a] = use[a] - ratio[b, a] * use[b]
        start = first if r + PIVOTS < 8 else first + 1
        for t in range(start, size // 8):
            tile = tiles[t]
            if t > first:
                cols = [spread(tile[:, j + a : j + a + 1]) for a in each]
            terms = [cols[a] * use[a] for a in each]
            while len(terms) > 1:
                terms = [x + y for x, y in zip(terms[::2], terms[1::2])]
            tiles[t] = jnp.where(at_any, 0.0, tile) - terms[0]
        top = jnp.where(sub < r, head, tiles[first])
        for a in each:
            top = jnp.where(sub == r + a, rows[a] * lax.rsqrt(pivots[a][a]), top)
        tiles[first] = top
    return jnp.concatenate(tiles, axis=0)


def inverse_kernel(size, total_rows, panels, gram_ref, out_ref, work, factor):
    full = gram_ref.shape[0]
    count = full // size
    wide = full // panels
    half = panels // 2
    work[...] = jnp.zeros_like(work)
    for low in range(panels):
        for high in range(low, panels):
            apart = high - low
            own, other = slice(low * wide, (low + 1) * wide), slice(high * wide, (high + 1) * wide)
            if not shared(panels, wide):
                work[own, other] = gram_ref[own, other] / total_rows
            elif apart < half:
                work[own, other] = gram_ref[own, apart * wide : (apart + 1) * wide] / total_rows
            elif apart > half:
                back = panels - apart
                part = gram_ref[other, back * wide : (back + 1) * wide] / total_rows
                work[own, other] = part.T
            else:
                middle = high * wide + wide // 2
                last = slice(half * wide, half * wide + wide // 2)
                work[own, high * wide : middle] = gram_ref[own, last] / total_rows
                work[own, middle : (high + 1) * wide] = gram_ref[other, last] / total_rows

    @pl.loop(0, count)
    def _(k):
        at = pl.multiple_of(k * size, size)
        done = factor_block(work[pl.ds(at, size), pl.ds(at, size)])
        down = lax.broadcasted_iota(jnp.int32, (size, size), 0)
        across = lax.broadcasted_iota(jnp.int32, (size, size), 1)
        factor[...] = jnp.where(across <= down, done, 0.0)
        for c in range(count):
            own = slice(c * size, (c + 1) * size)
            below = slice((c + 1) * size, full)

            @pl.when(k == c)
            def _():
                lower_inv = factor[...]
                left = slice(0, c * size)
                if c > 0:
                    out_ref[own, left] = jnp.dot(
                        lower_inv, work[own, left], precision=HIGHEST,
                        preferred_element_type=jnp.float32,
                    )
                out_ref[own, own] = lower_inv
                if c + 1 < count:
                    out_ref[own, below] = jnp.zeros((size, full - (c + 1) * size), jnp.float32)
                    right = jnp.dot(
                        lower_inv, work[own, below], precision=HIGHEST,
                        preferred_element_type=jnp.float32,
                    )
                    down_left = (((0,), (0,)), ((), ()))
                    work[below, below] -= lax.dot_general(
                        right, right, down_left, precision=HIGHEST,
                        preferred_element_type=jnp.float32,
                    )
                    known = slice(0, (c + 1) * size)
                    change = lax.dot_general(
                        right, out_ref[own, known], down_left, precision=HIGHEST,
                        preferred_element_type=jnp.float32,
                    )
                    if c > 0:
                        work[below, left] -= change[:, : c * size]
                    work[below, own] = -change[:, c * size :]


def shared(panels, wide):
    return panels % 2 == 0 and wide % 256 == 0


def panel_part(panel):
    panels, wide = lax.axis_size("vecs"), panel.shape[0]
    if not shared(panels, wide):
        return panel
    me, half, short = lax.axis_index("vecs"), panels // 2, wide // 2
    twice = jnp.concatenate([panel, panel], axis=1)
    near = lax.dynamic_slice_in_dim(twice, me * wide, half * wide, 1)
    far = lax.dynamic_slice_in_dim(twice, (me + half) * wide, wide, 1)
    middle = jnp.where(me < half, far[:, :short], far[short:, :].T)
    return jnp.concatenate([near, middle], axis=1)


def inverse_factor(gram, total_rows, panels):
    full = gram.shape[0]
    size = 128
    return pl.pallas_call(
        functools.partial(inverse_kernel, size, total_rows, panels),
        out_shape=jax.ShapeDtypeStruct((full, full), jnp.float32),
        in_specs=[pl.BlockSpec(memory_space=pltpu.VMEM)],
        out_specs=pl.BlockSpec(memory_space=pltpu.VMEM),
        scratch_shapes=[
            pltpu.VMEM((full, full), jnp.float32),
            pltpu.VMEM((size, size), jnp.float32),
        ],
        compiler_params=pltpu.CompilerParams(vmem_limit_bytes=VMEM_LIMIT),
        cost_estimate=pl.CostEstimate(
            flops=40 * full * full * full, bytes_accessed=8 * full * full, transcendentals=full
        ),
    )(gram)


def split_apply(left_bf, factor):
    factor_high = factor.astype(jnp.bfloat16)
    factor_low = (factor - factor_high.astype(jnp.float32)).astype(jnp.bfloat16)
    first = jnp.dot(left_bf, factor_high.T, preferred_element_type=jnp.float32)
    second = jnp.dot(left_bf, factor_low.T, preferred_element_type=jnp.float32)
    return first + second


def filtered_block(vectors, blocks, columns):
    block_rows, nnz, size_b = blocks.shape[:3]
    reach = block_rows // 4
    edge = reach * size_b
    first_row = lax.axis_index("rows") * block_rows
    local = columns - first_row
    edges_index = jnp.concatenate([local[:reach], local[block_rows - reach :]], axis=0) + reach
    edges_index = edges_index.reshape(-1)
    inner_index = local[reach : block_rows - reach].reshape(-1)
    inner_rows = block_rows - 2 * reach

    axis_size = lax.axis_size("rows")
    up = [(i, i + 1) for i in range(axis_size - 1)]
    down = [(j, i) for i, j in up]

    def inner_of(i, group):
        return i + reach // group

    def edges_of(i, group):
        return jnp.where(i < reach // group, i, i + inner_rows // group)

    def halves(array):
        return jnp.concatenate([array[:edge], array[-edge:]], axis=0), array[edge:-edge]

    cur_edges, cur_inner = halves(vectors)
    bf_edges, bf_inner = cur_edges, cur_inner
    old_edges = old_inner = None
    for iteration in range(DEGREE):
        kind = "first" if iteration == 0 else "next"
        emit_f32 = iteration < DEGREE - 1
        low, high = bf_edges[:edge], bf_edges[edge:]
        before = lax.ppermute(high, "rows", up)
        after = lax.ppermute(low, "rows", down)
        own = [low, bf_inner, high]
        new_inner = chebyshev_step(
            inner_index, own, blocks, inner_of, inner_rows, cur_inner, old_inner, kind, emit_f32
        )
        new_edges = chebyshev_step(
            edges_index, [before] + own + [after], blocks, edges_of, 2 * reach,
            cur_edges, old_edges, kind, emit_f32,
        )
        old_edges, old_inner = cur_edges, cur_inner
        bf_edges, bf_inner = new_edges[0], new_inner[0]
        if emit_f32:
            cur_edges, cur_inner = new_edges[1], new_inner[1]
    return jnp.concatenate([bf_edges[:edge], bf_inner, bf_edges[edge:]], axis=0)


def shards(vectors, blocks, columns):
    total_rows = vectors.shape[0] * lax.axis_size("rows")
    final = filtered_block(vectors, blocks, columns)
    panel_width = final.shape[1]
    whole_block = lax.all_gather(final, "vecs", axis=1, tiled=True)
    panel = lax.dot_general(
        final, whole_block, (((0,), (0,)), ((), ())), preferred_element_type=jnp.float32
    )
    summed = lax.psum(panel_part(panel), "rows")
    gram = lax.all_gather(summed, "vecs", axis=0, tiled=True)
    inverse = inverse_factor(gram, total_rows, lax.axis_size("vecs"))
    own_rows = lax.dynamic_slice_in_dim(
        inverse, lax.axis_index("vecs") * panel_width, panel_width, 0
    )
    return split_apply(whole_block, own_rows)


def solution(mesh):
    in_specs = (P("rows", "vecs"), P("rows", None, None, None), P("rows", None))
    out_specs = P("rows", "vecs")
    return jax.shard_map(shards, mesh=mesh, in_specs=in_specs, out_specs=out_specs, check_vma=False)
```
